32 devices in a mesh: expert: 4 (over z), fsdp: 8 (over y, x, core).
Axes of the slice: x: 2, y: 2, z: 4, core: 2. Of those that a mesh axis runs over, the one named last changes fastest.
Arguments:
- tokens: bfloat16 [8192, 2048], P(('expert', 'fsdp')), may hold values from -6 to 6
- cotangent: bfloat16 [8192, 2048], P(('expert', 'fsdp')), may hold values from -6 to 6
- routes: int32 [8192, 8], P(('expert', 'fsdp')), may hold values from 0 to 31, all different within a row; in each aligned block of 256 rows (0 to 255, 256 to 511, ...) at most 80 rows name the same one
- seq_lens: int32 [32, 8], P(('expert', 'fsdp')), may hold values from 1 to 128, 256 in all within a row
- attn_gain: float32 [2048], replicated, may hold values from 0.5 to 1.5
- q_gain: float32 [128], replicated, may hold values from 0.5 to 1.5
- key_norm_gain: float32 [128], replicated, may hold values from 0.5 to 1.5
- moe_gain: float32 [2048], replicated, may hold values from 0.5 to 1.5
- wq: bfloat16 [2048, 4096], P('fsdp'), may hold values from -0.125 to 0.125
- wk: bfloat16 [2048, 512], P('fsdp'), may hold values from -0.125 to 0.125
- wv: bfloat16 [2048, 512], P('fsdp'), may hold values from -0.125 to 0.125
- wo: bfloat16 [4096, 2048], P('fsdp'), may hold values from -0.5 to 0.5
- wr: bfloat16 [2048, 32], P('fsdp'), may hold values from -0.125 to 0.125
- w_gate: bfloat16 [32, 2048, 768], P(('expert', 'fsdp')), may hold values from -0.125 to 0.125
- w_up: bfloat16 [32, 2048, 768], P(('expert', 'fsdp')), may hold values from -0.125 to 0.125
- w_down: bfloat16 [32, 768, 2048], P(('expert', 'fsdp')), may hold values from -0.625 to 0.625
Outputs:
- layer_out: bfloat16 [8192, 2048], P(('expert', 'fsdp'))
- d_tokens: bfloat16 [8192, 2048], P(('expert', 'fsdp'))
- d_attn_gain: float32 [2048], replicated
- d_q_gain: float32 [128], replicated
- d_k_gain: float32 [128], replicated
- d_moe_gain: float32 [2048], replicated
- d_wq: float32 [2048, 4096], P('fsdp')
- d_wk: float32 [2048, 512], P('fsdp')
- d_wv: float32 [2048, 512], P('fsdp')
- d_wo: float32 [4096, 2048], P('fsdp')
- d_wr: float32 [2048, 32], P('fsdp')
- d_w_gate: float32 [32, 2048, 768], P(('expert', 'fsdp'))
- d_w_up: float32 [32, 2048, 768], P(('expert', 'fsdp'))
- d_w_down: float32 [32, 768, 2048], P(('expert', 'fsdp'))
The draws below stay inside these ranges and needn't reach their ends.
Inputs may be any that keep to these rules, and one draw needn't show every extreme that they name: `routes`: each row names 8 different experts. Among the rows of one device no expert is named more than 80 times, and some device names some expert exactly 80 times. `seq_lens`: each device's 8 lengths sum to 256, and the longest is exactly 128.
All inputs are finite; a program needn't handle non-finite values.
Results may differ from the reference program's by a relative error of at most 0.02.
Values may be sent and summed in bfloat16 or wider, within the bound.
No kernel may reach another device: no remote copies, remote signals or barrier semaphores. Data moves between devices by JAX's collectives and lax.ppermute only.
A program may use at most 384 MiB of HBM per device.

```python
import math
import jax
import jax.numpy as jnp
import numpy as np
from jax import lax

MODEL_WIDTH = 2048
QUERY_HEADS = 32
KEY_VALUE_HEADS = 4
HEAD_SIZE = 128
FF = 768
TOP = 8
SEGS = 8
TOK_DEV = 256
EXPERTS = 32
SEQ_MOST = 128
CAP = 80
TOKENS = 8192
N_EXPERT = 4
N_FSDP = 8


def level_of(key, dims, cuts, smallest, top_value):
    level = 1.0
    for axis_at, blocks in cuts:
        draws = jax.random.uniform(jax.random.fold_in(jax.random.fold_in(key, 6), axis_at), (blocks,), jnp.float32, smallest / len(cuts), top_value / len(cuts))
        level = level * jnp.repeat(jnp.exp(draws), dims[axis_at] // blocks).reshape((-1,) + (1,) * (len(dims) - 1 - axis_at))
    return level


def length_profile(number_of, total, most, lean):
    portions = [(1 << 20) // math.isqrt(grade ** lean) + 1 for grade in range(2, number_of + 1)]
    rest, given = total - most - (number_of - 1), [1] * (number_of - 1)
    while rest > 0:
        movable = [i for i in range(number_of - 1) if given[i] < most]
        whole, remaining = sum([portions[i] for i in movable]), rest
        for i in movable:
            addition = min(most - given[i], max(1, remaining * portions[i] // whole), rest)
            given[i] = given[i] + addition
            rest = rest - addition
    return np.array([most] + given)


def uneven_parts(stream_key, count, total, reach, slope):
    if count == 2:
        one = jax.random.randint(stream_key, (), max(1, total - reach), min(reach, total - 1) + 1)
        return jnp.stack([one, total - one])
    sizes = jnp.asarray(length_profile(count, total, reach, slope), jnp.int32)
    pairs = (count - 1) // 2
    giver, sink = sizes[1:1 + 2 * pairs:2], sizes[2:2 + 2 * pairs:2]
    room = jnp.minimum(giver - 1, reach - sink)
    shifted = jax.random.randint(jax.random.fold_in(stream_key, 1), (pairs,), 0, 1 << 20) % (room + 1)
    sizes = sizes.at[1:1 + 2 * pairs:2].set(giver - shifted).at[2:2 + 2 * pairs:2].set(sink + shifted)
    return sizes[jax.random.permutation(jax.random.fold_in(stream_key, 2), count)]


def assign_block(own_key, own, number, rows, number_of, top, reach, skew):
    order = jax.random.permutation(own_key, number_of)
    packed, ordinary = portions_of(number_of, rows * top, reach, skew, True), portions_of(number_of, rows * top, reach, skew, False)
    places = jnp.arange(number_of)

    def named(tallies, rotation):
        used = int((tallies > 0).sum())
        fixed = max(1, used // 4)
        passed = fixed + (places - fixed + rotation * (used - fixed)) % max(1, number_of - fixed)
        return jnp.zeros((number_of,), jnp.int32).at[order[jnp.where(places < fixed, places, passed)]].set(jnp.asarray(tallies, jnp.int32))

    tallies = jnp.where(number % 4 == 0, named(packed, number // 4), named(ordinary, number - number // 4 - 1))
    mixed = jax.random.permutation(jax.random.fold_in(own, 3), number_of)
    donor, sink = mixed[0:number_of // 2 * 2:2], mixed[1:number_of // 2 * 2:2]
    room = jnp.minimum(tallies[donor] - 1, reach - tallies[sink]) // 2
    room = jnp.where((donor == order[0]) | (sink == order[0]) | (tallies[sink] == 0), 0, jnp.maximum(room, 0))
    passed = jax.random.randint(jax.random.fold_in(own, 4), (number_of // 2,), 0, 1 << 20) % (room + 1)
    tallies = tallies.at[donor].add(-passed).at[sink].add(passed)
    members = jnp.searchsorted(jnp.cumsum(tallies), jnp.arange(rows * top), side="right").astype(jnp.int32)
    table = members.reshape(top, rows).T
    table = table[jax.random.permutation(jax.random.fold_in(own, 1), rows)]
    rotation = jax.random.randint(jax.random.fold_in(own, 2), (rows, 1), 0, top)
    return jnp.take_along_axis(table, (jnp.arange(top)[None, :] + rotation) % top, axis=1)


def portions_of(count, total, reach, slope, full):
    weights = [(1 << 20) // math.isqrt(grade ** slope) + 1 for grade in range(1, count + 1)]
    largest = reach if full else min(reach, max(-(-total // count), total * weights[0] // sum(weights)))
    least = 1 if total - largest >= count - 1 else 0
    holding, surplus = [largest] + [least] * (count - 1), total - largest - least * (count - 1)
    while surplus > 0:
        free = [i for i in range(1, count) if holding[i] < largest] or [i for i in range(1, count) if holding[i] < reach]
        pool, remaining = sum([weights[i] for i in free]), surplus
        for i in free:
            extra = min(reach - holding[i], max(1, remaining * weights[i] // pool), surplus)
            holding[i] = holding[i] + extra
            surplus = surplus - extra
    return np.array(holding)


def bell_draw(key, dims, scale, reach, shards=(), kind=jnp.bfloat16):
    entries = jax.random.normal(key, dims, jnp.float32) * scale
    if len(shards) > 0:
        entries = level_of(key, dims, shards, -0.22, 0.18) * entries
    return jnp.clip(entries, min=-reach, max=reach).astype(kind)


def setup_inputs(seed: int = 0) -> dict:
    key_list = jax.random.split(jax.random.key(seed), 17)
    tokens = bell_draw(key_list[0], (TOKENS, MODEL_WIDTH), 1.0, 6.0, ((0, 32),))
    cotangent = bell_draw(key_list[1], (TOKENS, MODEL_WIDTH), 1.0, 6.0, ((0, 32),))
    routes_keys = jax.random.split(jax.random.fold_in(key_list[2], 1), TOKENS // TOK_DEV)
    routes_turns = jax.random.permutation(jax.random.fold_in(key_list[2], 3), TOKENS // TOK_DEV)
    routes = jax.vmap(lambda own, number: assign_block(jax.random.fold_in(key_list[2], 2), own, number, TOK_DEV, EXPERTS, TOP, CAP, 2))(routes_keys, routes_turns).reshape((TOKENS, TOP))
    seq_lens = jax.vmap(lambda own: uneven_parts(own, SEGS, TOK_DEV, SEQ_MOST, 2))(jax.random.split(key_list[3], (N_EXPERT * N_FSDP))).reshape((N_EXPERT * N_FSDP, SEGS)).astype(jnp.int32)
    attn_gain = jnp.clip(1.0 + 0.1 * jax.random.normal(key_list[4], (MODEL_WIDTH,), jnp.float32), 0.5, 1.5)
    q_gain = jnp.clip(1.0 + 0.1 * jax.random.normal(key_list[5], (HEAD_SIZE,), jnp.float32), 0.5, 1.5)
    key_norm_gain = jnp.clip(1.0 + 0.1 * jax.random.normal(key_list[6], (HEAD_SIZE,), jnp.float32), 0.5, 1.5)
    moe_gain = jnp.clip(1.0 + 0.1 * jax.random.normal(key_list[7], (MODEL_WIDTH,), jnp.float32), 0.5, 1.5)
    wq = bell_draw(key_list[8], (MODEL_WIDTH, QUERY_HEADS * HEAD_SIZE), MODEL_WIDTH ** -0.5, 0.125, ((0, 8),))
    wk = bell_draw(key_list[9], (MODEL_WIDTH, KEY_VALUE_HEADS * HEAD_SIZE), MODEL_WIDTH ** -0.5, 0.125, ((0, 8),))
    wv = bell_draw(key_list[10], (MODEL_WIDTH, KEY_VALUE_HEADS * HEAD_SIZE), MODEL_WIDTH ** -0.5, 0.125, ((0, 8),))
    wo = bell_draw(key_list[11], (QUERY_HEADS * HEAD_SIZE, MODEL_WIDTH), (QUERY_HEADS * HEAD_SIZE // 32) ** -0.5, 0.5, ((0, 8),))
    wr = bell_draw(key_list[12], (MODEL_WIDTH, EXPERTS), MODEL_WIDTH ** -0.5, 0.125, ((0, 8),))
    w_gate = bell_draw(key_list[13], (EXPERTS, MODEL_WIDTH, FF), MODEL_WIDTH ** -0.5, 0.125, ((0, 32),))
    w_up = bell_draw(key_list[14], (EXPERTS, MODEL_WIDTH, FF), MODEL_WIDTH ** -0.5, 0.125, ((0, 32),))
    w_down = bell_draw(key_list[15], (EXPERTS, FF, MODEL_WIDTH), (FF // 8) ** -0.5, 0.625, ((0, 32),))
    return {"tokens": tokens, "cotangent": cotangent, "routes": routes, "seq_lens": seq_lens, "attn_gain": attn_gain, "q_gain": q_gain, "key_norm_gain": key_norm_gain, "moe_gain": moe_gain, "wq": wq, "wk": wk, "wv": wv, "wo": wo, "wr": wr, "w_gate": w_gate, "w_up": w_up, "w_down": w_down}


EPS = 1e-06
THETA = 1000000.0

def root_mean_norm(in_value, norm_gain):
    inverse = lax.rsqrt(lax.optimization_barrier(jnp.mean(in_value * in_value, axis=-1, keepdims=True)) + EPS)
    return in_value * inverse * norm_gain

def rotary_apply(in_value, rotary_angles):
    cosine = jnp.cos(rotary_angles)[:, None, :]
    sine = jnp.sin(rotary_angles)[:, None, :]
    half_size = in_value.shape[-1] // 2
    first = in_value[..., :half_size]
    second = in_value[..., half_size:]
    return jnp.concatenate([first * cosine - second * sine, second * cosine + first * sine], axis=-1)

def layout(lengths, token_count):
    ends = jnp.cumsum(lengths).astype(jnp.int32)
    index = jnp.arange(token_count, dtype=jnp.int32)
    segment = lax.optimization_barrier(jnp.sum((index[:, None] >= ends[None, :]).astype(jnp.int32), axis=1))
    starts = ends - lengths
    member = segment[:, None] == jnp.arange(lengths.shape[0], dtype=jnp.int32)[None, :]
    begins = lax.optimization_barrier(jnp.sum(jnp.where(member, starts[None, :], 0), axis=1)).astype(jnp.int32)
    position = (index - begins).astype(jnp.float32)
    allowed = (segment[:, None] == segment[None, :]) & (index[:, None] >= index[None, :])
    return (position, allowed)

def angles_of(position):
    exponent = jnp.arange(0, HEAD_SIZE, 2, dtype=jnp.float32) / HEAD_SIZE
    return position[:, None] * (THETA ** (-exponent))[None, :]

def heads_pre(q_proj, key_projection, q_gain, key_norm_gain, rotary_angles):
    token_count = q_proj.shape[0]
    query_rows = rotary_apply(root_mean_norm(q_proj.reshape(token_count, QUERY_HEADS, HEAD_SIZE), q_gain), rotary_angles)
    key_head_rows = rotary_apply(root_mean_norm(key_projection.reshape(token_count, KEY_VALUE_HEADS, HEAD_SIZE), key_norm_gain), rotary_angles)
    return (query_rows, key_head_rows)

def score_of(query_rows, key_head_rows, allowed):
    token_count = query_rows.shape[0]
    grouped_heads = query_rows.reshape(token_count, KEY_VALUE_HEADS, QUERY_HEADS // KEY_VALUE_HEADS, HEAD_SIZE).astype(jnp.float32)
    scores = jnp.einsum('qhgd,khd->hgqk', grouped_heads, key_head_rows.astype(jnp.float32)) * HEAD_SIZE ** (-0.5)
    return jnp.where(allowed[None, None], scores, -1e+30)

def attend(query_rows, key_head_rows, value_rows, allowed):
    token_count = query_rows.shape[0]
    scores = score_of(query_rows, key_head_rows, allowed)
    row_max = lax.optimization_barrier(jnp.max(scores, axis=-1, keepdims=True))
    unnormed = jnp.where(allowed[None, None], jnp.exp(scores - row_max), 0.0)
    summed = lax.optimization_barrier(jnp.sum(unnormed, axis=-1, keepdims=True))
    log_total = row_max + jnp.log(summed)
    probs = jnp.where(allowed[None, None], jnp.exp(scores - log_total), 0.0).astype(jnp.bfloat16)
    mixed = jnp.einsum('hgqk,khd->qhgd', probs.astype(jnp.float32), value_rows.astype(jnp.float32))
    return (mixed.reshape(token_count, QUERY_HEADS * HEAD_SIZE).astype(jnp.bfloat16), log_total)

def attend_back(query_rows, key_head_rows, value_rows, head_output, head_gradient, log_total, allowed):
    token_count = query_rows.shape[0]
    scores = score_of(query_rows, key_head_rows, allowed)
    prob_f = jnp.where(allowed[None, None], jnp.exp(scores - log_total), 0.0)
    prob_b = prob_f.astype(jnp.bfloat16).astype(jnp.float32)
    output_gradients = head_gradient.reshape(token_count, KEY_VALUE_HEADS, QUERY_HEADS // KEY_VALUE_HEADS, HEAD_SIZE).astype(jnp.float32)
    output_rows = head_output.reshape(token_count, KEY_VALUE_HEADS, QUERY_HEADS // KEY_VALUE_HEADS, HEAD_SIZE).astype(jnp.float32)
    value_gradient = jnp.einsum('hgqk,qhgd->khd', prob_b, output_gradients)
    d_prob = jnp.einsum('qhgd,khd->hgqk', output_gradients, value_rows.astype(jnp.float32))
    delta = jnp.transpose(lax.optimization_barrier(jnp.sum(output_gradients * output_rows, axis=-1)), (1, 2, 0))[..., None]
    d_scores = (prob_f * (d_prob - delta) * HEAD_SIZE ** (-0.5)).astype(jnp.bfloat16).astype(jnp.float32)
    d_query = jnp.einsum('hgqk,khd->qhgd', d_scores, key_head_rows.astype(jnp.float32))
    grouped_heads = query_rows.reshape(token_count, KEY_VALUE_HEADS, QUERY_HEADS // KEY_VALUE_HEADS, HEAD_SIZE).astype(jnp.float32)
    d_key = jnp.einsum('hgqk,qhgd->khd', d_scores, grouped_heads)
    return (d_query.reshape(token_count, QUERY_HEADS, HEAD_SIZE), d_key, value_gradient)

def forward_block(layer_block, lengths, attn_gain, q_gain, key_norm_gain, wq, wk, wv, wo):
    token_count = layer_block.shape[0]
    position, allowed = layout(lengths, token_count)
    rotary_angles = angles_of(position)
    x_f = layer_block.astype(jnp.float32)
    x_norm = root_mean_norm(x_f, attn_gain).astype(jnp.bfloat16)
    q_proj = jnp.dot(x_norm, wq, preferred_element_type=jnp.float32)
    key_projection = jnp.dot(x_norm, wk, preferred_element_type=jnp.float32)
    value_projection = jnp.dot(x_norm, wv, preferred_element_type=jnp.float32)

    def pre_fn(q_in, k_in, qg_in, kg_in):
        return heads_pre(q_in, k_in, qg_in, kg_in, rotary_angles)
    (query_f, key_f), heads_back = jax.vjp(pre_fn, q_proj, key_projection, q_gain, key_norm_gain)
    query_rows = query_f.astype(jnp.bfloat16)
    key_head_rows = key_f.astype(jnp.bfloat16)
    value_rows = value_projection.reshape(token_count, KEY_VALUE_HEADS, HEAD_SIZE).astype(jnp.bfloat16)
    head_output, log_total = attend(query_rows, key_head_rows, value_rows, allowed)
    resid = x_f + jnp.dot(head_output, wo, preferred_element_type=jnp.float32)
    return (resid, x_f, x_norm, query_rows, key_head_rows, value_rows, head_output, log_total, allowed, heads_back)

def reference(tokens, cotangent, routes, seq_lens, attn_gain, q_gain, key_norm_gain, moe_gain, wq, wk, wv, wo, wr, w_gate, w_up, w_down):
    num_dev = N_EXPERT * N_FSDP
    total_tok = num_dev * TOK_DEV
    width = tokens.shape[1]
    tok_blocks = tokens.reshape(num_dev, TOK_DEV, width)

    def section_one(carry, blocks_in):
        layer_block, lengths = blocks_in
        outs_fwd = forward_block(layer_block, lengths, attn_gain, q_gain, key_norm_gain, wq, wk, wv, wo)
        resid = outs_fwd[0]
        moe_in = root_mean_norm(resid, moe_gain).astype(jnp.bfloat16)
        return (carry, (resid, moe_in))
    _, (resid_all, moe_all) = lax.scan(section_one, jnp.zeros((), jnp.float32), (tok_blocks, seq_lens))
    resid_all = resid_all.reshape(total_tok, width)
    moe_in = moe_all.reshape(total_tok, width)
    logits = jnp.dot(moe_in, wr, preferred_element_type=jnp.float32)
    routed = jnp.take_along_axis(logits, routes, axis=1)
    gates = jax.nn.softmax(routed, axis=1)
    pairs = routes.reshape(num_dev, TOK_DEV * TOP)

    def slots_of(row_routes):
        hits = (row_routes[:, None] == jnp.arange(EXPERTS, dtype=jnp.int32)[None, :]).astype(jnp.int32)
        return lax.optimization_barrier(jnp.sum((jnp.cumsum(hits, axis=0) - 1) * hits, axis=1)).astype(jnp.int32)
    slots = lax.map(slots_of, pairs)
    device_of = jnp.arange(num_dev, dtype=jnp.int32)[:, None]
    within = jnp.arange(TOK_DEV * TOP, dtype=jnp.int32)[None, :]
    column = (device_of * CAP + slots).reshape(-1)
    token_id = (device_of * TOK_DEV + within // TOP).reshape(-1)
    pair_id = (device_of * (TOK_DEV * TOP) + within).reshape(-1)
    flat_routes = pairs.reshape(-1)
    table = jnp.full((EXPERTS, num_dev * CAP), total_tok, jnp.int32).at[flat_routes, column].set(token_id)
    pair_table = jnp.full((EXPERTS, num_dev * CAP), total_tok * TOP, jnp.int32).at[flat_routes, column].set(pair_id)
    moe_pad = jnp.concatenate([moe_in, jnp.zeros((1, width), jnp.bfloat16)], axis=0)
    d_out = cotangent.astype(jnp.float32)
    d_out_pad = jnp.concatenate([d_out, jnp.zeros((1, width), jnp.float32)], axis=0)
    gate_pad = jnp.concatenate([gates.reshape(-1), jnp.zeros((1,), jnp.float32)], axis=0)

    def expert_step(carry, expert_in):
        mix_sum, d_gate_sum, d_moe_sum = carry
        gate_mat, up_mat, down_mat, rows_id, pair_idx = expert_in
        rows_in = moe_pad[rows_id]
        gate_pre = jnp.dot(rows_in, gate_mat, preferred_element_type=jnp.float32)
        up_pre = jnp.dot(rows_in, up_mat, preferred_element_type=jnp.float32)
        sigma = jax.nn.sigmoid(gate_pre)
        active = gate_pre * sigma
        hidden = (active * up_pre).astype(jnp.bfloat16)
        result = jnp.dot(hidden, down_mat, preferred_element_type=jnp.float32).astype(jnp.bfloat16)
        result_f = result.astype(jnp.float32)
        gate_rows = gate_pad[pair_idx]
        grad_rows = d_out_pad[rows_id]
        mix_sum = mix_sum.at[rows_id].add(gate_rows[:, None] * result_f)
        d_gate_sum = d_gate_sum.at[pair_idx].add(lax.optimization_barrier(jnp.sum(grad_rows * result_f, axis=1)))
        d_expert = (gate_rows[:, None] * grad_rows).astype(jnp.bfloat16)
        d_hidden = jnp.dot(d_expert, down_mat.T, preferred_element_type=jnp.float32)
        d_gate_pre = (d_hidden * up_pre * sigma * (1.0 + gate_pre * (1.0 - sigma))).astype(jnp.bfloat16)
        d_up_pre = (d_hidden * active).astype(jnp.bfloat16)
        grad_down = jnp.dot(hidden.T, d_expert, preferred_element_type=jnp.float32)
        grad_gate = jnp.dot(rows_in.T, d_gate_pre, preferred_element_type=jnp.float32)
        grad_up = jnp.dot(rows_in.T, d_up_pre, preferred_element_type=jnp.float32)
        d_back = (jnp.dot(d_gate_pre, gate_mat.T, preferred_element_type=jnp.float32) + jnp.dot(d_up_pre, up_mat.T, preferred_element_type=jnp.float32)).astype(jnp.bfloat16)
        d_moe_sum = d_moe_sum.at[rows_id].add(d_back.astype(jnp.float32))
        return ((mix_sum, d_gate_sum, d_moe_sum), (grad_gate, grad_up, grad_down))
    init = (jnp.zeros((total_tok + 1, width), jnp.float32), jnp.zeros((total_tok * TOP + 1,), jnp.float32), jnp.zeros((total_tok + 1, width), jnp.float32))
    (mix_sum, d_gate_sum, d_moe_sum), (d_w_gate, d_w_up, d_w_down) = lax.scan(expert_step, init, (w_gate, w_up, w_down, table, pair_table))
    layer_out = (resid_all + mix_sum[:total_tok]).astype(jnp.bfloat16)
    d_gates = d_gate_sum[:total_tok * TOP].reshape(total_tok, TOP)
    d_routed = gates * (d_gates - lax.optimization_barrier(jnp.sum(gates * d_gates, axis=1, keepdims=True)))
    chosen = routes[:, :, None] == jnp.arange(EXPERTS, dtype=jnp.int32)[None, None, :]
    d_logits = lax.optimization_barrier(jnp.sum(jnp.where(chosen, d_routed[:, :, None], 0.0), axis=1))
    d_wr = jnp.dot(moe_in.astype(jnp.float32).T, d_logits, precision=lax.Precision.HIGHEST)
    d_moe_in = d_moe_sum[:total_tok] + jnp.dot(d_logits, wr.astype(jnp.float32).T, precision=lax.Precision.HIGHEST)

    def section_two(carry, blocks_in):
        g_attn, g_query, g_key, g_moe, g_wq, g_wk, g_wv, g_wo = carry
        layer_block, lengths, d_moe_blk, dy_blk = blocks_in
        resid, x_f, x_norm, query_rows, key_head_rows, value_rows, head_output, log_total, allowed, heads_back = forward_block(layer_block, lengths, attn_gain, q_gain, key_norm_gain, wq, wk, wv, wo)
        _, moe_back = jax.vjp(root_mean_norm, resid, moe_gain)
        d_resid_norm, d_moe_gain = moe_back(d_moe_blk)
        d_resid = dy_blk + d_resid_norm
        d_attn = d_resid.astype(jnp.bfloat16)
        g_wo = g_wo + jnp.dot(head_output.T, d_attn, preferred_element_type=jnp.float32)
        head_gradient = jnp.dot(d_attn, wo.T, preferred_element_type=jnp.float32).astype(jnp.bfloat16)
        d_query, d_key, value_gradient = attend_back(query_rows, key_head_rows, value_rows, head_output, head_gradient, log_total, allowed)
        d_q_proj, d_k_proj, d_q_gain, d_k_gain = heads_back((d_query, d_key))
        d_q_b = d_q_proj.astype(jnp.bfloat16)
        d_k_b = d_k_proj.astype(jnp.bfloat16)
        value_block_gradient = value_gradient.reshape(layer_block.shape[0], KEY_VALUE_HEADS * HEAD_SIZE).astype(jnp.bfloat16)
        g_wq = g_wq + jnp.dot(x_norm.T, d_q_b, preferred_element_type=jnp.float32)
        g_wk = g_wk + jnp.dot(x_norm.T, d_k_b, preferred_element_type=jnp.float32)
        g_wv = g_wv + jnp.dot(x_norm.T, value_block_gradient, preferred_element_type=jnp.float32)
        d_x_norm = jnp.dot(d_q_b, wq.T, preferred_element_type=jnp.float32) + jnp.dot(d_k_b, wk.T, preferred_element_type=jnp.float32) + jnp.dot(value_block_gradient, wv.T, preferred_element_type=jnp.float32)
        _, attn_back = jax.vjp(root_mean_norm, x_f, attn_gain)
        d_x_pre, d_attn_gain = attn_back(d_x_norm)
        d_block = (d_resid + d_x_pre).astype(jnp.bfloat16)
        carry = (g_attn + d_attn_gain, g_query + d_q_gain, g_key + d_k_gain, g_moe + d_moe_gain, g_wq, g_wk, g_wv, g_wo)
        return (carry, d_block)
    init_two = (jnp.zeros((width,), jnp.float32), jnp.zeros((HEAD_SIZE,), jnp.float32), jnp.zeros((HEAD_SIZE,), jnp.float32), jnp.zeros((width,), jnp.float32), jnp.zeros(wq.shape, jnp.float32), jnp.zeros(wk.shape, jnp.float32), jnp.zeros(wv.shape, jnp.float32), jnp.zeros(wo.shape, jnp.float32))
    (g_attn, g_query, g_key, g_moe, g_wq, g_wk, g_wv, g_wo), d_blocks = lax.scan(section_two, init_two, (tok_blocks, seq_lens, d_moe_in.reshape(num_dev, TOK_DEV, width), d_out.reshape(num_dev, TOK_DEV, width)))
    d_tokens = d_blocks.reshape(total_tok, width)
    return (layer_out, d_tokens, g_attn, g_query, g_key, g_moe, g_wq, g_wk, g_wv, g_wo, d_wr, d_w_gate, d_w_up, d_w_down)
```

```python
import jax
import jax.numpy as jnp
from jax import lax
from jax.sharding import PartitionSpec as P

QUERY_HEADS = 32
KEY_VALUE_HEADS = 4
HEAD_SIZE = 128


EPS = 1e-06
THETA = 1000000.0


def root_mean_norm(in_value, norm_gain):
    inverse = lax.rsqrt(jnp.mean(in_value * in_value, axis=-1, keepdims=True) + EPS)
    return in_value * inverse * norm_gain


def rotary_apply(in_value, rotary_angles):
    cosine = jnp.cos(rotary_angles)[:, None, :]
    sine = jnp.sin(rotary_angles)[:, None, :]
    half_size = in_value.shape[-1] // 2
    first = in_value[..., :half_size]
    second = in_value[..., half_size:]
    return jnp.concatenate(
        [first * cosine - second * sine, second * cosine + first * sine], axis=-1
    )


def layout(lengths, token_count):
    ends = jnp.cumsum(lengths)
    index = jnp.arange(token_count, dtype=jnp.int32)
    segment = jnp.sum((index[:, None] >= ends[None, :]).astype(jnp.int32), axis=1)
    starts = ends - lengths
    member = segment[:, None] == jnp.arange(lengths.shape[0], dtype=jnp.int32)[None, :]
    begins = jnp.sum(jnp.where(member, starts[None, :], 0), axis=1)
    position = (index - begins).astype(jnp.float32)
    allowed = (segment[:, None] == segment[None, :]) & (index[:, None] >= index[None, :])
    return (position, allowed)


def angles_of(position):
    exponent = jnp.arange(0, HEAD_SIZE, 2, dtype=jnp.float32) / HEAD_SIZE
    return position[:, None] * (THETA ** (-exponent))[None, :]


def heads_pre(q_proj, key_projection, q_gain, key_norm_gain, rotary_angles):
    token_count = q_proj.shape[0]
    query_rows = rotary_apply(
        root_mean_norm(q_proj.reshape(token_count, QUERY_HEADS, HEAD_SIZE), q_gain), rotary_angles
    )
    key_head_rows = rotary_apply(
        root_mean_norm(
            key_projection.reshape(token_count, KEY_VALUE_HEADS, HEAD_SIZE), key_norm_gain
        ),
        rotary_angles,
    )
    return (query_rows, key_head_rows)


def back_dot(left, right):
    return lax.dot_general(
        left, right, (((1,), (1,)), ((), ())), preferred_element_type=jnp.float32
    )


def score_of(query_rows, key_head_rows, allowed):
    token_count = query_rows.shape[0]
    grouped_heads = query_rows.reshape(
        token_count, KEY_VALUE_HEADS, QUERY_HEADS // KEY_VALUE_HEADS, HEAD_SIZE
    )
    scores = jnp.einsum(
        "qhgd,khd->hgqk", grouped_heads, key_head_rows, preferred_element_type=jnp.float32
    ) * HEAD_SIZE ** (-0.5)
    return jnp.where(allowed[None, None], scores, -1e30)


def attend(query_rows, key_head_rows, value_rows, allowed):
    token_count = query_rows.shape[0]
    scores = score_of(query_rows, key_head_rows, allowed)
    row_max = jnp.max(scores, axis=-1, keepdims=True)
    unnormed = jnp.where(allowed[None, None], jnp.exp(scores - row_max), 0.0)
    summed = jnp.sum(unnormed, axis=-1, keepdims=True)
    log_total = row_max + jnp.log(summed)
    probs = jnp.where(allowed[None, None], jnp.exp(scores - log_total), 0.0).astype(jnp.bfloat16)
    mixed = jnp.einsum("hgqk,khd->qhgd", probs, value_rows, preferred_element_type=jnp.float32)
    return (mixed.reshape(token_count, QUERY_HEADS * HEAD_SIZE).astype(jnp.bfloat16), log_total)


def attend_back(
    query_rows, key_head_rows, value_rows, head_output, head_gradient, log_total, allowed
):
    token_count = query_rows.shape[0]
    scores = score_of(query_rows, key_head_rows, allowed)
    prob_f = jnp.where(allowed[None, None], jnp.exp(scores - log_total), 0.0)
    prob_b = prob_f.astype(jnp.bfloat16)
    output_gradients = head_gradient.reshape(
        token_count, KEY_VALUE_HEADS, QUERY_HEADS // KEY_VALUE_HEADS, HEAD_SIZE
    )
    output_rows = head_output.reshape(
        token_count, KEY_VALUE_HEADS, QUERY_HEADS // KEY_VALUE_HEADS, HEAD_SIZE
    )
    value_gradient = jnp.einsum(
        "hgqk,qhgd->khd", prob_b, output_gradients, preferred_element_type=jnp.float32
    )
    d_prob = jnp.einsum(
        "qhgd,khd->hgqk", output_gradients, value_rows, preferred_element_type=jnp.float32
    )
    delta = jnp.sum(output_gradients.astype(jnp.float32) * output_rows.astype(jnp.float32), axis=-1)
    delta = jnp.transpose(delta, (1, 2, 0))[..., None]
    d_scores = (prob_f * (d_prob - delta) * HEAD_SIZE ** (-0.5)).astype(jnp.bfloat16)
    d_query = jnp.einsum(
        "hgqk,khd->qhgd", d_scores, key_head_rows, preferred_element_type=jnp.float32
    )
    grouped_heads = query_rows.reshape(
        token_count, KEY_VALUE_HEADS, QUERY_HEADS // KEY_VALUE_HEADS, HEAD_SIZE
    )
    d_key = jnp.einsum(
        "hgqk,qhgd->khd", d_scores, grouped_heads, preferred_element_type=jnp.float32
    )
    return (d_query.reshape(token_count, QUERY_HEADS, HEAD_SIZE), d_key, value_gradient)


def route_places(ids, wanted):
    hit = jnp.any(ids[..., :, None, :] == wanted[:, None], axis=-3)
    tokens = ids.shape[-1]
    before = jnp.triu(jnp.ones((tokens, tokens), jnp.bfloat16), 1)
    slots = jnp.dot(hit.astype(jnp.bfloat16), before, preferred_element_type=jnp.float32)
    return jnp.where(hit, slots, -1.0)


def dot32(left, right):
    return jnp.dot(left, right, preferred_element_type=jnp.float32)


def first_dot(left, right):
    return lax.dot_general(
        left, right, (((0,), (0,)), ((), ())), preferred_element_type=jnp.float32
    )


def body(
    tokens,
    cotangent,
    routes,
    seq_lens,
    attn_gain,
    q_gain,
    key_norm_gain,
    moe_gain,
    wq,
    wk,
    wv,
    wo,
    wr,
    w_gate,
    w_up,
    w_down,
):
    token_count, width = tokens.shape
    experts = wr.shape[1]
    top_k = routes.shape[1]
    n_exp = lax.axis_size("expert")
    n_fsdp = lax.axis_size("fsdp")
    everyone = ("expert", "fsdp")
    cap = max(2, token_count * top_k * 5 // (4 * experts))
    plane = lax.axis_index("expert")
    column = lax.axis_index("fsdp")
    rel = range(n_exp)
    bf = jnp.bfloat16

    def across(value, r):
        return lax.ppermute(value, "expert", [(i, i ^ r) for i in range(n_exp)]) if r else value

    def in_plane(value):
        return lax.all_to_all(value, "fsdp", split_axis=0, concat_axis=0, tiled=True)

    routes_t = routes.T
    routes_all = lax.all_gather(routes_t, everyone, axis=0, tiled=True)
    routes_all = routes_all.reshape(n_exp, n_fsdp, top_k, token_count)
    planes_rel = jnp.arange(n_exp, dtype=jnp.int32) ^ plane
    routes_rel = jnp.take(routes_all, planes_rel, axis=0)
    routes_col = lax.dynamic_index_in_dim(routes_rel, column, 1, keepdims=False)
    plane_experts = plane * n_fsdp + jnp.arange(n_fsdp, dtype=jnp.int32)
    slot_ids = jnp.arange(cap, dtype=jnp.int32).astype(jnp.float32)
    col_places = route_places(routes_col, plane_experts)
    picks = (col_places[:, :, None, :] == slot_ids[:, None]).astype(bf)
    picks = picks.reshape(n_exp, n_fsdp * cap, token_count)
    own_expert = plane * n_fsdp + column
    expert_places = route_places(routes_rel, own_expert[None])[:, :, 0, :]
    own_places = route_places(routes_t, jnp.arange(experts, dtype=jnp.int32))

    def dispatch(value):
        out = []
        for r in rel:
            rows = dot32(picks[r], across(value, r)).astype(bf)
            out.append(in_plane(rows.reshape(n_fsdp, cap, width)).reshape(n_fsdp * cap, width))
        return out

    def combine(parts):
        total = None
        for r in rel:
            back = in_plane(parts[r].reshape(n_fsdp, cap, width)).reshape(n_fsdp * cap, width)
            summed = first_dot(picks[r], back)
            if r:
                summed = across(summed.astype(bf), r).astype(jnp.float32)
            total = summed if total is None else total + summed
        return total

    grad_rows = dispatch(cotangent)

    position, allowed = layout(seq_lens[0], token_count)
    rotary_angles = angles_of(position)
    x_f = tokens.astype(jnp.float32)
    x_norm_f, attn_back = jax.vjp(root_mean_norm, x_f, attn_gain)
    x_norm = x_norm_f.astype(bf)
    q_cols = wq.shape[1]
    k_cols = wk.shape[1]
    pad = -experts % 128
    packed = jnp.concatenate([wq, wk, wv, jnp.pad(wr, ((0, 0), (0, pad)))], axis=1)
    w_in = lax.all_gather(packed, "fsdp", axis=0, tiled=True)
    wr_all = w_in[:, q_cols + 2 * k_cols : q_cols + 2 * k_cols + experts]
    wo_all = lax.all_gather(wo, "fsdp", axis=0, tiled=True)
    proj = dot32(x_norm, w_in)
    q_proj = proj[:, :q_cols]
    key_projection = proj[:, q_cols : q_cols + k_cols]
    value_projection = proj[:, q_cols + k_cols : q_cols + 2 * k_cols]

    def pre_fn(q_in, k_in, qg_in, kg_in):
        return heads_pre(q_in, k_in, qg_in, kg_in, rotary_angles)

    (query_f, key_f), heads_back = jax.vjp(pre_fn, q_proj, key_projection, q_gain, key_norm_gain)
    query_rows = query_f.astype(bf)
    key_head_rows = key_f.astype(bf)
    value_rows = value_projection.reshape(token_count, KEY_VALUE_HEADS, HEAD_SIZE).astype(bf)
    head_output, log_total = attend(query_rows, key_head_rows, value_rows, allowed)
    resid = x_f + dot32(head_output, wo_all)
    moe_norm, moe_back = jax.vjp(root_mean_norm, resid, moe_gain)
    moe_in = moe_norm.astype(bf)

    flat_in = dispatch(moe_in)
    logits = lax.dot_general(
        wr_all, moe_in, (((0,), (1,)), ((), ())), preferred_element_type=jnp.float32
    )
    chosen = own_places >= 0.0
    top_logit = jnp.max(jnp.where(chosen, logits, -jnp.inf), axis=0, keepdims=True)
    raised = jnp.where(chosen, jnp.exp(jnp.where(chosen, logits - top_logit, 0.0)), 0.0)
    gates = raised / jnp.sum(raised, axis=0, keepdims=True)
    gates_all = lax.all_gather(gates, everyone, axis=0, tiled=True)
    gates_all = gates_all.reshape(n_exp, n_fsdp, experts, token_count)
    gate_own = lax.dynamic_index_in_dim(gates_all, own_expert, 2, keepdims=False)
    gate_own = jnp.take(gate_own, planes_rel, axis=0)
    slot_gates = jnp.sum(
        jnp.where(expert_places[:, :, None, :] == slot_ids[:, None], gate_own[:, :, None, :], 0.0),
        axis=3,
    )
    gate_mat = w_gate[0]
    up_mat = w_up[0]
    down_mat = w_down[0]
    back_parts, out_parts, hid_parts, dg_parts, du_parts, gate_grads = [], [], [], [], [], []
    for r in rel:
        gate_pre = dot32(flat_in[r], gate_mat)
        up_pre = dot32(flat_in[r], up_mat)
        d_plain = back_dot(grad_rows[r], down_mat)
        scale = slot_gates[r].reshape(-1, 1)
        sigma = jax.nn.sigmoid(gate_pre)
        active = gate_pre * sigma
        hidden = active * up_pre
        gate_grads.append(
            jnp.sum(hidden.astype(bf).astype(jnp.float32) * d_plain, axis=1).reshape(n_fsdp, cap)
        )
        d_hidden = d_plain * scale
        d_gate_pre = (d_hidden * up_pre * sigma * (1.0 + gate_pre * (1.0 - sigma))).astype(bf)
        d_up_pre = (d_hidden * active).astype(bf)
        hidden_scaled = (hidden * scale).astype(bf)
        back_parts.append((back_dot(d_gate_pre, gate_mat) + back_dot(d_up_pre, up_mat)).astype(bf))
        out_parts.append(dot32(hidden_scaled, down_mat).astype(bf))
        hid_parts.append(hidden_scaled)
        dg_parts.append(d_gate_pre)
        du_parts.append(d_up_pre)
    d_moe_in = combine(back_parts)
    gate_grads = jnp.take(jnp.stack(gate_grads), planes_rel, axis=0)
    gate_grads = lax.all_gather(gate_grads.reshape(n_exp * n_fsdp, cap), everyone, axis=0, tiled=True)
    gate_grads = gate_grads.reshape(experts, n_exp * n_fsdp, cap)
    gate_grads = lax.dynamic_index_in_dim(gate_grads, own_expert, 1, keepdims=False)
    d_gates = jnp.sum(
        jnp.where(own_places[:, None, :] == slot_ids[:, None], gate_grads[:, :, None], 0.0), axis=1
    )
    d_logits = gates * (d_gates - jnp.sum(gates * d_gates, axis=0, keepdims=True))
    d_moe_in = d_moe_in + lax.dot_general(
        d_logits,
        wr_all.astype(jnp.float32),
        (((0,), (1,)), ((), ())),
        precision=lax.Precision.HIGHEST,
        preferred_element_type=jnp.float32,
    )
    d_out = cotangent.astype(jnp.float32)
    d_resid_norm, d_moe_gain = moe_back(d_moe_in)
    d_resid = d_out + d_resid_norm
    d_attn = d_resid.astype(bf)

    d_attn_all = lax.all_gather(d_attn, "fsdp", axis=0, tiled=True)
    d_logits_all = lax.all_gather(d_logits, "fsdp", axis=0, tiled=True)
    x_norm_all = lax.all_gather(x_norm, "fsdp", axis=0, tiled=True)
    heads_cols = lax.all_to_all(head_output, "fsdp", split_axis=1, concat_axis=0, tiled=True)
    moe_cols = lax.all_to_all(moe_in, "fsdp", split_axis=1, concat_axis=0, tiled=True)
    head_gradient = back_dot(d_attn, wo_all).astype(bf)
    d_query, d_key, value_gradient = attend_back(
        query_rows, key_head_rows, value_rows, head_output, head_gradient, log_total, allowed
    )
    d_q_proj, d_k_proj, d_q_gain, d_k_gain = heads_back((d_query, d_key))
    d_q_b = d_q_proj.astype(bf)
    d_k_b = d_k_proj.astype(bf)
    d_v_b = value_gradient.reshape(token_count, k_cols).astype(bf)
    d_proj = jnp.concatenate(
        [d_q_b, d_k_b, d_v_b, jnp.zeros((token_count, experts + pad), bf)], axis=1
    )
    d_x_norm = back_dot(d_proj, w_in)
    d_x_pre, d_attn_gain = attn_back(d_x_norm)
    d_tokens = (d_resid + d_x_pre).astype(bf)

    grad_outproj = first_dot(heads_cols, d_attn_all)
    q_part = q_cols // n_fsdp
    k_part = k_cols // n_fsdp
    d_cols = jnp.concatenate(
        [
            d_q_b.reshape(token_count, n_fsdp, q_part),
            d_k_b.reshape(token_count, n_fsdp, k_part),
            d_v_b.reshape(token_count, n_fsdp, k_part),
        ],
        axis=2,
    ).reshape(token_count, -1)
    d_cols = lax.all_to_all(d_cols, "fsdp", split_axis=1, concat_axis=0, tiled=True)
    grad_in = first_dot(x_norm_all, d_cols).astype(bf)
    grad_in = lax.all_to_all(grad_in, "fsdp", split_axis=0, concat_axis=1, tiled=True)
    d_logits_all = d_logits_all.reshape(n_fsdp, experts, token_count)
    d_logits_all = jnp.transpose(d_logits_all, (1, 0, 2)).reshape(experts, n_fsdp * token_count)
    grad_router = lax.dot_general(
        moe_cols.astype(jnp.float32),
        d_logits_all,
        (((0,), (1,)), ((), ())),
        precision=lax.Precision.HIGHEST,
        preferred_element_type=jnp.float32,
    )
    grad_outproj = lax.psum(grad_outproj.astype(bf), "expert").astype(jnp.float32)
    grad_router = jnp.pad(grad_router.astype(bf), ((0, 0), (0, pad)))
    grad_rows_in = jnp.concatenate([grad_in, grad_router], axis=1)
    grad_rows_in = lax.psum(grad_rows_in, "expert").astype(jnp.float32)
    in_cols = n_fsdp * (q_part + 2 * k_part)
    split = grad_rows_in[:, :in_cols].reshape(-1, n_fsdp, q_part + 2 * k_part)
    grad_query = split[:, :, :q_part].reshape(-1, q_cols)
    grad_key = split[:, :, q_part : q_part + k_part].reshape(-1, k_cols)
    grad_value = split[:, :, q_part + k_part :].reshape(-1, k_cols)
    grad_router = grad_rows_in[:, in_cols : in_cols + experts]

    rows_in = jnp.concatenate(flat_in, axis=0)
    grad_gate = first_dot(rows_in, jnp.concatenate(dg_parts, axis=0))
    grad_up = first_dot(rows_in, jnp.concatenate(du_parts, axis=0))
    grad_down = first_dot(jnp.concatenate(hid_parts, axis=0), jnp.concatenate(grad_rows, axis=0))
    layer_out = (resid + combine(out_parts)).astype(bf)
    gain_sums = lax.psum((d_attn_gain, d_q_gain, d_k_gain, d_moe_gain), everyone)
    return (
        layer_out,
        d_tokens,
        gain_sums[0],
        gain_sums[1],
        gain_sums[2],
        gain_sums[3],
        grad_query,
        grad_key,
        grad_value,
        grad_outproj,
        grad_router,
        grad_gate[None],
        grad_up[None],
        grad_down[None],
    )


def solution(mesh):
    in_specs = (
        P(("expert", "fsdp"), None),
        P(("expert", "fsdp"), None),
        P(("expert", "fsdp"), None),
        P(("expert", "fsdp"), None),
        P(),
        P(),
        P(),
        P(),
        P("fsdp", None),
        P("fsdp", None),
        P("fsdp", None),
        P("fsdp", None),
        P("fsdp", None),
        P(("expert", "fsdp"), None, None),
        P(("expert", "fsdp"), None, None),
        P(("expert", "fsdp"), None, None),
    )
    out_specs = (
        P(("expert", "fsdp"), None),
        P(("expert", "fsdp"), None),
        P(),
        P(),
        P(),
        P(),
        P("fsdp", None),
        P("fsdp", None),
        P("fsdp", None),
        P("fsdp", None),
        P("fsdp", None),
        P(("expert", "fsdp"), None, None),
        P(("expert", "fsdp"), None, None),
        P(("expert", "fsdp"), None, None),
    )
    return jax.shard_map(body, mesh=mesh, in_specs=in_specs, out_specs=out_specs, check_vma=False)
```

```python
import jax
import jax.numpy as jnp
from jax import lax
from jax.sharding import PartitionSpec as P

QUERY_HEADS = 32
KEY_VALUE_HEADS = 4
HEAD_SIZE = 128


EPS = 1e-06
THETA = 1000000.0


def root_mean_norm(in_value, norm_gain):
    inverse = lax.rsqrt(jnp.mean(in_value * in_value, axis=-1, keepdims=True) + EPS)
    return in_value * inverse * norm_gain


def rotary_apply(in_value, rotary_angles):
    cosine = jnp.cos(rotary_angles)[:, None, :]
    sine = jnp.sin(rotary_angles)[:, None, :]
    half_size = in_value.shape[-1] // 2
    first = in_value[..., :half_size]
    second = in_value[..., half_size:]
    return jnp.concatenate(
        [first * cosine - second * sine, second * cosine + first * sine], axis=-1
    )


def layout(lengths, token_count):
    ends = jnp.cumsum(lengths)
    index = jnp.arange(token_count, dtype=jnp.int32)
    segment = jnp.sum((index[:, None] >= ends[None, :]).astype(jnp.int32), axis=1)
    starts = ends - lengths
    member = segment[:, None] == jnp.arange(lengths.shape[0], dtype=jnp.int32)[None, :]
    begins = jnp.sum(jnp.where(member, starts[None, :], 0), axis=1)
    position = (index - begins).astype(jnp.float32)
    allowed = (segment[:, None] == segment[None, :]) & (index[:, None] >= index[None, :])
    return (position, allowed)


def angles_of(position):
    exponent = jnp.arange(0, HEAD_SIZE, 2, dtype=jnp.float32) / HEAD_SIZE
    return position[:, None] * (THETA ** (-exponent))[None, :]


def heads_pre(q_proj, key_projection, q_gain, key_norm_gain, rotary_angles):
    token_count = q_proj.shape[0]
    query_rows = rotary_apply(
        root_mean_norm(q_proj.reshape(token_count, QUERY_HEADS, HEAD_SIZE), q_gain), rotary_angles
    )
    key_head_rows = rotary_apply(
        root_mean_norm(
            key_projection.reshape(token_count, KEY_VALUE_HEADS, HEAD_SIZE), key_norm_gain
        ),
        rotary_angles,
    )
    return (query_rows, key_head_rows)


def back_dot(left, right):
    return lax.dot_general(
        left, right, (((1,), (1,)), ((), ())), preferred_element_type=jnp.float32
    )


def score_of(query_rows, key_head_rows, allowed):
    token_count = query_rows.shape[0]
    grouped_heads = query_rows.reshape(
        token_count, KEY_VALUE_HEADS, QUERY_HEADS // KEY_VALUE_HEADS, HEAD_SIZE
    )
    scores = jnp.einsum(
        "qhgd,khd->hgqk", grouped_heads, key_head_rows, preferred_element_type=jnp.float32
    ) * HEAD_SIZE ** (-0.5)
    return jnp.where(allowed[None, None], scores, -1e30)


def attend(query_rows, key_head_rows, value_rows, allowed):
    token_count = query_rows.shape[0]
    scores = score_of(query_rows, key_head_rows, allowed)
    row_max = jnp.max(scores, axis=-1, keepdims=True)
    unnormed = jnp.where(allowed[None, None], jnp.exp(scores - row_max), 0.0)
    summed = jnp.sum(unnormed, axis=-1, keepdims=True)
    log_total = row_max + jnp.log(summed)
    probs = jnp.where(allowed[None, None], jnp.exp(scores - log_total), 0.0).astype(jnp.bfloat16)
    mixed = jnp.einsum("hgqk,khd->qhgd", probs, value_rows, preferred_element_type=jnp.float32)
    return (mixed.reshape(token_count, QUERY_HEADS * HEAD_SIZE).astype(jnp.bfloat16), log_total)


def attend_back(
    query_rows, key_head_rows, value_rows, head_output, head_gradient, log_total, allowed
):
    token_count = query_rows.shape[0]
    scores = score_of(query_rows, key_head_rows, allowed)
    prob_f = jnp.where(allowed[None, None], jnp.exp(scores - log_total), 0.0)
    prob_b = prob_f.astype(jnp.bfloat16)
    output_gradients = head_gradient.reshape(
        token_count, KEY_VALUE_HEADS, QUERY_HEADS // KEY_VALUE_HEADS, HEAD_SIZE
    )
    output_rows = head_output.reshape(
        token_count, KEY_VALUE_HEADS, QUERY_HEADS // KEY_VALUE_HEADS, HEAD_SIZE
    )
    value_gradient = jnp.einsum(
        "hgqk,qhgd->khd", prob_b, output_gradients, preferred_element_type=jnp.float32
    )
    d_prob = jnp.einsum(
        "qhgd,khd->hgqk", output_gradients, value_rows, preferred_element_type=jnp.float32
    )
    delta = jnp.sum(output_gradients.astype(jnp.float32) * output_rows.astype(jnp.float32), axis=-1)
    delta = jnp.transpose(delta, (1, 2, 0))[..., None]
    d_scores = (prob_f * (d_prob - delta) * HEAD_SIZE ** (-0.5)).astype(jnp.bfloat16)
    d_query = jnp.einsum(
        "hgqk,khd->qhgd", d_scores, key_head_rows, preferred_element_type=jnp.float32
    )
    grouped_heads = query_rows.reshape(
        token_count, KEY_VALUE_HEADS, QUERY_HEADS // KEY_VALUE_HEADS, HEAD_SIZE
    )
    d_key = jnp.einsum(
        "hgqk,qhgd->khd", d_scores, grouped_heads, preferred_element_type=jnp.float32
    )
    return (d_query.reshape(token_count, QUERY_HEADS, HEAD_SIZE), d_key, value_gradient)


def route_places(ids, wanted):
    hit = jnp.any(ids[..., :, None, :] == wanted[:, None], axis=-3)
    tokens = ids.shape[-1]
    before = jnp.triu(jnp.ones((tokens, tokens), jnp.bfloat16), 1)
    slots = jnp.dot(hit.astype(jnp.bfloat16), before, preferred_element_type=jnp.float32)
    return jnp.where(hit, slots, -1.0)


def return_order(n_exp):
    half = max(1, n_exp // 2)
    return list(range(half, n_exp)) + list(range(half))


def dot32(left, right):
    return jnp.dot(left, right, preferred_element_type=jnp.float32)


def first_dot(left, right):
    return lax.dot_general(
        left, right, (((0,), (0,)), ((), ())), preferred_element_type=jnp.float32
    )


def layer(
    tokens,
    cotangent,
    routes,
    seq_lens,
    attn_gain,
    q_gain,
    key_norm_gain,
    moe_gain,
    wq,
    wk,
    wv,
    wo,
    wr,
    w_gate,
    w_up,
    w_down,
):
    token_count, width = tokens.shape
    experts = wr.shape[1]
    top_k = routes.shape[1]
    n_exp = lax.axis_size("expert")
    n_fsdp = lax.axis_size("fsdp")
    cap = max(2, token_count * top_k * 5 // (4 * experts))
    plane = lax.axis_index("expert")
    rel = range(n_exp)
    back_order = return_order(n_exp)
    bf = jnp.bfloat16

    def across(value, r):
        return lax.ppermute(value, "expert", [(i, i ^ r) for i in range(n_exp)])

    def in_plane(value, split=0, concat=0):
        return lax.all_to_all(value, "fsdp", split_axis=split, concat_axis=concat, tiled=True)

    def gathered(value):
        return lax.all_gather(value, "fsdp", axis=0, tiled=True)

    def with_notes(rows, notes):
        flat = jnp.concatenate([note.reshape(-1) for note in notes]).astype(bf)
        lines = -(-flat.shape[0] // (8 * width)) * 8
        flat = jnp.pad(flat, (0, lines * width - flat.shape[0]))
        return jnp.concatenate([rows, flat.reshape(lines, width)], axis=0)

    def note_of(rows, number):
        first = token_count * width + number * n_fsdp * token_count
        line, rest = first // width, n_fsdp * token_count
        lines = -(-rest // width)
        if first % width == 0 and rest % width == 0:
            flat = rows[line : line + lines].reshape(-1)
        else:
            flat = rows.reshape(-1)[first : first + rest]
        return flat.astype(jnp.float32).reshape(n_fsdp, token_count)

    def halves(value):
        high = value.astype(bf)
        return [high, (value - high.astype(jnp.float32)).astype(bf)]

    planes_rel = jnp.arange(n_exp, dtype=jnp.int32) ^ plane
    own_places = route_places(routes.T, jnp.arange(experts, dtype=jnp.int32))
    places_rel = jnp.take(own_places.reshape(n_exp, n_fsdp, token_count), planes_rel, axis=0)
    slot_ids = jnp.arange(cap, dtype=jnp.int32).astype(jnp.float32)
    col_places, picks, grad_rows = [], [], []
    for r in rel:
        rows = cotangent
        places = places_rel[0]
        if r:
            rows = across(with_notes(cotangent, [places_rel[r]]), r)
            places = note_of(rows, 0)
            rows = rows[:token_count]
        pick = (places[:, None, :] == slot_ids[:, None]).astype(bf)
        pick = pick.reshape(n_fsdp * cap, token_count)
        col_places.append(places)
        picks.append(pick)
        rows = dot32(pick, rows).astype(bf).reshape(n_fsdp, cap, width)
        grad_rows.append(in_plane(rows).reshape(n_fsdp * cap, width))

    position, allowed = layout(seq_lens[0], token_count)
    rotary_angles = angles_of(position)
    x_f = tokens.astype(jnp.float32)
    x_norm_f, attn_back = jax.vjp(root_mean_norm, x_f, attn_gain)
    x_norm = x_norm_f.astype(bf)
    q_cols = wq.shape[1]
    k_cols = wk.shape[1]
    pad = -experts % 128
    packed = jnp.concatenate([wq, wk, wv, jnp.pad(wr, ((0, 0), (0, pad)))], axis=1)
    w_in = gathered(packed)
    wr_all = w_in[:, q_cols + 2 * k_cols : q_cols + 2 * k_cols + experts]
    wo_all = gathered(wo)
    x_in, *early = lax.optimization_barrier((x_norm, *grad_rows[: n_exp - 1]))
    grad_rows = early + grad_rows[n_exp - 1 :]
    proj = dot32(x_in, w_in)
    q_proj = proj[:, :q_cols]
    key_projection = proj[:, q_cols : q_cols + k_cols]
    value_projection = proj[:, q_cols + k_cols : q_cols + 2 * k_cols]

    def pre_fn(q_in, k_in, qg_in, kg_in):
        return heads_pre(q_in, k_in, qg_in, kg_in, rotary_angles)

    (query_f, key_f), heads_back = jax.vjp(pre_fn, q_proj, key_projection, q_gain, key_norm_gain)
    query_rows = query_f.astype(bf)
    key_head_rows = key_f.astype(bf)
    value_rows = value_projection.reshape(token_count, KEY_VALUE_HEADS, HEAD_SIZE).astype(bf)
    head_output, log_total = attend(query_rows, key_head_rows, value_rows, allowed)
    head_output, grad_rows[-1] = lax.optimization_barrier((head_output, grad_rows[-1]))
    resid = x_f + dot32(head_output, wo_all)
    moe_norm, moe_back = jax.vjp(root_mean_norm, resid, moe_gain)
    moe_in = moe_norm.astype(bf)

    logits = lax.dot_general(
        wr_all, moe_in, (((0,), (1,)), ((), ())), preferred_element_type=jnp.float32
    )
    chosen = own_places >= 0.0
    top_logit = jnp.max(jnp.where(chosen, logits, -jnp.inf), axis=0, keepdims=True)
    raised = jnp.where(chosen, jnp.exp(jnp.where(chosen, logits - top_logit, 0.0)), 0.0)
    gates = raised / jnp.sum(raised, axis=0, keepdims=True)
    gates_rel = jnp.take(gates.reshape(n_exp, n_fsdp, token_count), planes_rel, axis=0)
    flat_in, slot_gates = [], []
    for r in rel:
        rows = moe_in
        gate_rows = gates_rel[0]
        if r:
            rows = across(with_notes(moe_in, halves(gates_rel[r])), r)
            gate_rows = note_of(rows, 0) + note_of(rows, 1)
            rows = rows[:token_count]
        rows = dot32(picks[r], rows).astype(bf).reshape(n_fsdp, cap, width)
        flat_in.append(in_plane(rows).reshape(n_fsdp * cap, width))
        found = col_places[r][:, None, :] == slot_ids[:, None]
        slot_gates.append(jnp.sum(jnp.where(found, gate_rows[:, None, :], 0.0), axis=2))
    half = max(1, n_exp // 2)
    slot_gates = [
        part
        for first in range(0, n_exp, half)
        for part in in_plane(jnp.stack(slot_gates[first : first + half], axis=1))
        .transpose(1, 0, 2)
        .reshape(half, n_fsdp * cap, 1)
    ]
    gate_mat = w_gate[0]
    up_mat = w_up[0]
    down_mat = w_down[0]
    back_parts, out_parts, hid_parts, dg_parts, du_parts, gate_grads = [], [], [], [], [], []
    for r in rel:
        gate_pre = dot32(flat_in[r], gate_mat)
        up_pre = dot32(flat_in[r], up_mat)
        d_plain = back_dot(grad_rows[r], down_mat)
        scale = slot_gates[r]
        sigma = jax.nn.sigmoid(gate_pre)
        active = gate_pre * sigma
        hidden = active * up_pre
        gate_grads.append(
            jnp.sum(hidden.astype(bf).astype(jnp.float32) * d_plain, axis=1).reshape(n_fsdp, cap)
        )
        d_hidden = d_plain * scale
        d_gate_pre = (d_hidden * up_pre * sigma * (1.0 + gate_pre * (1.0 - sigma))).astype(bf)
        d_up_pre = (d_hidden * active).astype(bf)
        hidden_scaled = (hidden * scale).astype(bf)
        back_parts.append((back_dot(d_gate_pre, gate_mat) + back_dot(d_up_pre, up_mat)).astype(bf))
        out_parts.append(dot32(hidden_scaled, down_mat).astype(bf))
        hid_parts.append(hidden_scaled)
        dg_parts.append(d_gate_pre)
        du_parts.append(d_up_pre)
    gate_grads = in_plane(jnp.stack(gate_grads, axis=1))
    d_gates = [None] * n_exp
    d_moe_in = None
    for r in back_order:
        back = in_plane(back_parts[r].reshape(n_fsdp, cap, width))
        summed = first_dot(picks[r], back.reshape(n_fsdp * cap, width))
        found = col_places[r][:, None, :] == slot_ids[:, None]
        gate_part = jnp.sum(jnp.where(found, gate_grads[:, r, :, None], 0.0), axis=1)
        if r:
            rows = across(with_notes(summed.astype(bf), halves(gate_part)), r)
            gate_part = note_of(rows, 0) + note_of(rows, 1)
            summed = rows[:token_count].astype(jnp.float32)
        d_moe_in = summed if d_moe_in is None else d_moe_in + summed
        d_gates[r] = gate_part
    d_gates = jnp.take(jnp.stack(d_gates), planes_rel, axis=0).reshape(experts, token_count)
    d_logits = gates * (d_gates - jnp.sum(gates * d_gates, axis=0, keepdims=True))
    d_moe_in = d_moe_in + lax.dot_general(
        d_logits,
        wr_all.astype(jnp.float32),
        (((0,), (1,)), ((), ())),
        precision=lax.Precision.HIGHEST,
        preferred_element_type=jnp.float32,
    )
    d_out = cotangent.astype(jnp.float32)
    d_resid_norm, d_moe_gain = moe_back(d_moe_in)
    d_resid = d_out + d_resid_norm
    d_attn = d_resid.astype(bf)

    d_attn_all = gathered(d_attn)
    x_norm_all = gathered(x_norm)
    heads_cols = in_plane(head_output, 1, 0)
    grad_router = lax.dot_general(
        d_logits,
        moe_in.astype(jnp.float32),
        (((1,), (0,)), ((), ())),
        precision=lax.Precision.HIGHEST,
        preferred_element_type=jnp.float32,
    )
    grad_router = grad_router.reshape(experts, n_fsdp, width // n_fsdp).transpose(1, 0, 2)
    grad_router = jnp.sum(in_plane(grad_router), axis=0).T
    head_gradient = back_dot(d_attn, wo_all).astype(bf)
    d_query, d_key, value_gradient = attend_back(
        query_rows, key_head_rows, value_rows, head_output, head_gradient, log_total, allowed
    )
    d_q_proj, d_k_proj, d_q_gain, d_k_gain = heads_back((d_query, d_key))
    d_q_b = d_q_proj.astype(bf)
    d_k_b = d_k_proj.astype(bf)
    d_v_b = value_gradient.reshape(token_count, k_cols).astype(bf)
    d_proj = jnp.concatenate(
        [d_q_b, d_k_b, d_v_b, jnp.zeros((token_count, experts + pad), bf)], axis=1
    )
    d_x_norm = back_dot(d_proj, w_in)
    d_x_pre, d_attn_gain = attn_back(d_x_norm)
    d_tokens = (d_resid + d_x_pre).astype(bf)

    grad_outproj = first_dot(heads_cols, d_attn_all)
    q_part = q_cols // n_fsdp
    k_part = k_cols // n_fsdp
    d_cols = jnp.concatenate(
        [
            d_q_b.reshape(token_count, n_fsdp, q_part),
            d_k_b.reshape(token_count, n_fsdp, k_part),
            d_v_b.reshape(token_count, n_fsdp, k_part),
        ],
        axis=2,
    ).reshape(token_count, -1)
    d_cols = in_plane(d_cols, 1, 0)
    grad_in = first_dot(x_norm_all, d_cols).astype(bf)
    grad_in = in_plane(grad_in, 0, 1)
    grad_outproj = lax.psum(grad_outproj.astype(bf), "expert")
    grad_router = jnp.pad(grad_router.astype(bf), ((0, 0), (0, pad)))
    grad_rows_in = jnp.concatenate([grad_in, grad_router], axis=1)
    grad_rows_in, grad_outproj = lax.optimization_barrier((grad_rows_in, grad_outproj))
    grad_outproj = grad_outproj.astype(jnp.float32)
    grad_rows_in = lax.psum(grad_rows_in, "expert").astype(jnp.float32)
    in_cols = n_fsdp * (q_part + 2 * k_part)
    split = grad_rows_in[:, :in_cols].reshape(-1, n_fsdp, q_part + 2 * k_part)
    grad_query = split[:, :, :q_part].reshape(-1, q_cols)
    grad_key = split[:, :, q_part : q_part + k_part].reshape(-1, k_cols)
    grad_value = split[:, :, q_part + k_part :].reshape(-1, k_cols)
    grad_router = grad_rows_in[:, in_cols : in_cols + experts]

    rows_in = jnp.concatenate(flat_in, axis=0)
    grad_gate = first_dot(rows_in, jnp.concatenate(dg_parts, axis=0))
    grad_up = first_dot(rows_in, jnp.concatenate(du_parts, axis=0))
    grad_down = first_dot(jnp.concatenate(hid_parts, axis=0), jnp.concatenate(grad_rows, axis=0))
    mixed = resid
    for r in back_order:
        back = in_plane(out_parts[r].reshape(n_fsdp, cap, width))
        summed = first_dot(picks[r], back.reshape(n_fsdp * cap, width))
        if r:
            summed = across(summed.astype(bf), r).astype(jnp.float32)
        mixed = mixed + summed
    layer_out = mixed.astype(bf)
    gains = [d_attn_gain, d_q_gain, d_k_gain, d_moe_gain]
    sizes = [gain.shape[0] for gain in gains]
    gain_rows = jnp.concatenate(gains).reshape(-1, HEAD_SIZE)
    gain_rows = jnp.broadcast_to(gain_rows, (n_fsdp,) + gain_rows.shape)
    gain_rows = jnp.sum(in_plane(gain_rows), axis=0)
    by_plane = jnp.stack([across(gain_rows, r) if r else gain_rows for r in rel])
    gain_rows = jnp.sum(jnp.take(by_plane, planes_rel, axis=0), axis=0).reshape(-1)
    gain_sums, at = [], 0
    for size in sizes:
        gain_sums.append(gain_rows[at : at + size])
        at += size
    return (
        layer_out,
        d_tokens,
        gain_sums[0],
        gain_sums[1],
        gain_sums[2],
        gain_sums[3],
        grad_query,
        grad_key,
        grad_value,
        grad_outproj,
        grad_router,
        grad_gate[None],
        grad_up[None],
        grad_down[None],
    )


def solution(mesh):
    in_specs = (
        P(("expert", "fsdp"), None),
        P(("expert", "fsdp"), None),
        P(("expert", "fsdp"), None),
        P(("expert", "fsdp"), None),
        P(),
        P(),
        P(),
        P(),
        P("fsdp", None),
        P("fsdp", None),
        P("fsdp", None),
        P("fsdp", None),
        P("fsdp", None),
        P(("expert", "fsdp"), None, None),
        P(("expert", "fsdp"), None, None),
        P(("expert", "fsdp"), None, None),
    )
    out_specs = (
        P(("expert", "fsdp"), None),
        P(("expert", "fsdp"), None),
        P(),
        P(),
        P(),
        P(),
        P("fsdp", None),
        P("fsdp", None),
        P("fsdp", None),
        P("fsdp", None),
        P("fsdp", None),
        P(("expert", "fsdp"), None, None),
        P(("expert", "fsdp"), None, None),
        P(("expert", "fsdp"), None, None),
    )
    return jax.shard_map(layer, mesh=mesh, in_specs=in_specs, out_specs=out_specs, check_vma=False)
```
